32 devices in a mesh: groups: 2 (over y), frame: 4 (over x, core), row: 4 (over z).
Axes of the slice: x: 2, y: 2, z: 4, core: 2. Of those that a mesh axis runs over, the one named last changes fastest.
Arguments:
- observed: float32 [16, 128, 2048], P('frame', ('groups', 'row')), parts along dimension 1, may hold values from 0.5 to 8
- kernels: float32 [8, 5], replicated, may hold values from 0.05 to 1
- band_kernel: int32 [16], P('groups'), parts along dimension 0, may hold values from 0 to 7
- masks: int32 [256, 128, 16], P(None, ('groups', 'row'), 'frame'), parts along dimension 1, may hold values from 0 to 1, as said below
Outputs:
- spikes: bfloat16 [16, 128, 2048], P(None, ('groups', 'row'), 'frame'), parts along dimension 1
- traces: float32 [512, 16], P(('groups', 'frame', 'row')), parts along dimension 0
The draws below stay inside these ranges and needn't reach their ends.
There are 2 independent parts, one for each index of `groups`. The reference program is written for one: setup_inputs(seed, part) draws one part's arguments, and reference() takes and returns one part's arrays. A program takes and returns all parts, laid end to end along the dimension named above; an argument that names none is the same for every part. Nothing has to cross between parts.
Inputs may be any that keep to these rules, and one draw needn't show every extreme that they name: `masks`: each component covers the tile at its centre and a random half of the tiles within 8 rows and one tile column of that centre, so it covers at least one tile.
All inputs are finite; a program needn't handle non-finite values.
Results may differ from the reference program's by a relative error of at most 0.0062.
Values may be sent and summed in bfloat16 or wider, within the bound.
A program may use at most 64 MiB of HBM per device.

```python
import math
import jax
import jax.numpy as jnp
from jax import lax

W = 2048
K = 256
TILE = 128
TAPS = 5
NK = 8
BAND = 8
REACH = 8
ITERS = 3
F = 16
H = 64
NT = 16


def draw_masks(key, part):
    key_row, key_col, key_coin = jax.random.split(key, 3)
    centre_row = jax.random.randint(key_row, (K,), 0, H)
    centre_col = jax.random.randint(key_col, (K,), 0, NT)
    coin_flips = jax.random.randint(key_coin, (K, H, NT), 0, 2)
    row_ids = jnp.arange(H)[None, :, None]
    col_ids = jnp.arange(NT)[None, None, :]
    row_gap = jnp.abs(row_ids - centre_row[:, None, None])
    col_gap = jnp.abs(col_ids - centre_col[:, None, None])
    nearby = (row_gap <= REACH) & (col_gap <= 1) & (coin_flips == 1)
    centre = (row_gap == 0) & (col_gap == 0)
    return jnp.where(nearby | centre, 1, 0).astype(jnp.int32)


def plant(array, key, smallest, top_value):
    place = [jax.random.randint(jax.random.fold_in(key, axis), (), 0, length) for axis, length in enumerate(array.shape)]
    longest = array.shape.index(max(array.shape))
    neighbour = place[:longest] + [(place[longest] + 1) % array.shape[longest]] + place[longest + 1:]
    return array.at[tuple(place)].set(smallest).at[tuple(neighbour)].set(top_value)


def levels(rng, shape, shards, low, high):
    loudness, own = 1.0, jax.random.fold_in(rng, 6)
    for dim, shards_of in shards:
        steps = jnp.exp(jax.random.uniform(jax.random.fold_in(own, dim), (shards_of,), jnp.float32, low / len(shards), high / len(shards)))
        loudness = loudness * jnp.repeat(steps, shape[dim] // shards_of).reshape([-1 if axis == dim else 1 for axis in range(len(shape))])
    return loudness


def setup_inputs(seed: int = 0, part: int = 0) -> dict:
    streams_of = jax.random.split(jax.random.key(seed), 5)
    part_splits = jax.random.split(jax.random.fold_in(streams_of[4], part), 5)
    return {
        "observed": jnp.clip(jnp.exp(math.log(8.0) - 2.7725887 * jax.random.uniform(part_splits[0], (F, H, W), jnp.float32) ** levels(part_splits[0], (F, H, W), ((0, 4), (1, 4)), -0.2, 0.2)), 0.5, 8.0),
        "kernels": jnp.clip(jnp.exp(jax.random.uniform(streams_of[1], (NK, TAPS), jnp.float32, math.log(0.05), math.log(1.0))), 0.05, 1.0),
        "band_kernel": plant(jax.random.randint(part_splits[2], (H // BAND,), 0, NK), jax.random.fold_in(part_splits[2], 1), 0, NK - 1).astype(jnp.int32),
        "masks": draw_masks(jax.random.fold_in(jax.random.fold_in(streams_of[4], part), 71), part),
    }


SMOOTHING = 1024.0
DECAY_RATE = 0.9

def table_rows(kernels, band_kernel):
    tap_table = kernels / jnp.sum(kernels, axis=1, keepdims=True)
    row_bands = jnp.arange(H) // BAND
    return tap_table[band_kernel[row_bands]]

def restore_image(image, row_taps):
    padded_taps = jnp.pad(row_taps, ((2, 2), (0, 0)))
    current = image
    for iteration in range(ITERS):
        padded = jnp.pad(current, ((2, 2), (0, 0)))
        blurred = row_taps[:, 0:1] * padded[0:H]
        for offset in range(1, 5):
            blurred = blurred + row_taps[:, offset:offset + 1] * padded[offset:offset + H]
        quotient = image / blurred
        padded_quotient = jnp.pad(quotient, ((2, 2), (0, 0)))
        back = padded_taps[4:4 + H, 0:1] * padded_quotient[4:4 + H]
        for offset in range(1, 5):
            start = 4 - offset
            back = back + padded_taps[start:start + H, offset:offset + 1] * padded_quotient[start:start + H]
        current = current * back
    return current.astype(jnp.bfloat16)

def smooth_series(series):
    values = series.astype(jnp.float32)
    frame_total = values.shape[0]
    frame_ids = jnp.arange(frame_total)
    at_ends = (frame_ids == 0) | (frame_ids == frame_total - 1)
    middle = (1.0 + SMOOTHING * jnp.where(at_ends, 1.0, 2.0)).astype(jnp.float32)
    sub_diag = jnp.where(frame_ids == 0, 0.0, -SMOOTHING).astype(jnp.float32)
    super_diag = jnp.where(frame_ids == frame_total - 1, 0.0, -SMOOTHING).astype(jnp.float32)
    baseline = lax.linalg.tridiagonal_solve(sub_diag, middle, super_diag, values)
    detrended = values - baseline
    earlier = jnp.concatenate([jnp.zeros((1, values.shape[1]), jnp.float32), detrended[:-1]], axis=0)
    return (detrended - DECAY_RATE * earlier).astype(jnp.bfloat16)

def reference(observed, kernels, band_kernel, masks):
    row_taps = table_rows(kernels, band_kernel)
    estimate = lax.map(lambda image: restore_image(image, row_taps), observed)
    by_rows = jnp.transpose(estimate, (1, 0, 2))
    spikes = jnp.transpose(lax.map(smooth_series, by_rows), (1, 0, 2))
    tile_sums = jnp.sum(spikes.astype(jnp.float32).reshape(F, H, NT, TILE), axis=3)
    weights = masks.astype(jnp.float32)
    trace_sums = jnp.einsum('khc,fhc->kf', weights, tile_sums, precision=lax.Precision.HIGHEST)
    counts = jnp.sum(weights, axis=(1, 2))
    traces = trace_sums / (TILE * counts[:, None])
    return (spikes, traces)
```

```python
import functools
import jax
import jax.numpy as jnp
from jax import lax
from jax.experimental import pallas as pl
from jax.experimental.pallas import tpu as pltpu
from jax.sharding import PartitionSpec as P

TILE = 128
BAND = 8
ITERS = 3
REACH = 2
HALO = 2 * REACH * ITERS
OWN = 16

SMOOTHING = 1024.0
DECAY_RATE = 0.9


def thomas_factors(frames):
    inverse, upper = [], []
    for t in range(frames):
        diag = 1.0 + SMOOTHING * (1.0 if t in (0, frames - 1) else 2.0)
        pivot = diag if t == 0 else diag + SMOOTHING * upper[-1]
        inverse.append(1.0 / pivot)
        upper.append(-SMOOTHING / pivot)
    return inverse, upper


def body(cfg, obs_hbm, kern_ref, band_ref, masks_hbm, spikes_ref, traces_ref,
         obs, cur, quo, taps, outm, send, est, masks, wide, wt, rhs, part, gath,
         load_sem, mask_sem, zs, zr, fs, fr, rs, rr):
    nf, nr, fd, rows, cpd, comps = cfg
    ct_n = cpd // TILE
    frames = fd * nf
    nd = nf * nr
    brows = rows + 2 * OWN
    slot = rhs_slot(frames)
    pack = TILE // slot
    kdev = comps // nd
    kq = kdev // pack
    f = lax.axis_index("frame")
    r = lax.axis_index("row")
    me = f * nr + r

    def chunk_of(s):
        dx = s // 2 + 1
        return ((f // 2 + dx) % (nf // 2)) * 2 + (f % 2 + 1 + s) % 2

    def load(s, ct):
        col = pl.multiple_of(chunk_of(s) * cpd + ct * TILE, TILE)
        return pltpu.make_async_copy(
            obs_hbm.at[:, :, pl.ds(col, TILE)],
            obs.at[s, :, ct, OWN : OWN + rows, :],
            load_sem.at[s, ct],
        )

    def up(s):
        return pltpu.make_async_remote_copy(
            src_ref=obs.at[s, :, :, OWN : OWN + HALO, :],
            dst_ref=obs.at[s, :, :, OWN + rows : OWN + rows + HALO, :],
            send_sem=zs.at[0, s],
            recv_sem=zr.at[0, s],
            device_id={"row": r - 1},
            device_id_type=pl.DeviceIdType.MESH,
        )

    def down(s):
        return pltpu.make_async_remote_copy(
            src_ref=obs.at[s, :, :, OWN + rows - HALO : OWN + rows, :],
            dst_ref=obs.at[s, :, :, OWN - HALO : OWN, :],
            send_sem=zs.at[1, s],
            recv_sem=zr.at[1, s],
            device_id={"row": r + 1},
            device_id_type=pl.DeviceIdType.MESH,
        )

    def frame_copy(s):
        c = chunk_of(s)
        return pltpu.make_async_remote_copy(
            src_ref=send.at[s],
            dst_ref=est.at[f],
            send_sem=fs.at[s],
            recv_sem=fr.at[f],
            device_id={"frame": c},
            device_id_type=pl.DeviceIdType.MESH,
        )

    def frame_wait(s):
        c = chunk_of(s)
        return pltpu.make_async_remote_copy(
            src_ref=send.at[s],
            dst_ref=est.at[c],
            send_sem=fs.at[s],
            recv_sem=fr.at[c],
            device_id={"frame": c},
            device_id_type=pl.DeviceIdType.MESH,
        )

    def part_copy(off):
        d = (me + off) % nd
        return pltpu.make_async_remote_copy(
            src_ref=part.at[d],
            dst_ref=gath.at[me],
            send_sem=rs.at[d],
            recv_sem=rr.at[me],
            device_id={"frame": d // nr, "row": d % nr},
            device_id_type=pl.DeviceIdType.MESH,
        )

    def part_wait(off):
        d = (me + off) % nd
        return pltpu.make_async_remote_copy(
            src_ref=part.at[d],
            dst_ref=gath.at[d],
            send_sem=rs.at[d],
            recv_sem=rr.at[d],
            device_id={"frame": d // nr, "row": d % nr},
            device_id_type=pl.DeviceIdType.MESH,
        )

    barrier = pltpu.get_barrier_semaphore()

    def greet(off, _):
        d = (me + off) % nd
        pl.semaphore_signal(
            barrier, inc=1, device_id={"frame": d // nr, "row": d % nr},
            device_id_type=pl.DeviceIdType.MESH,
        )
        return 0

    lax.fori_loop(1, nd, greet, 0)

    def start_loads(s, _):
        for ct in range(ct_n):
            load(s, ct).start()
        return 0

    lax.fori_loop(0, nf, start_loads, 0)
    mask_copy = pltpu.make_async_copy(masks_hbm, masks, mask_sem)
    mask_copy.start()

    bands = band_ref.shape[0]
    for b in range(brows // BAND):
        band = r * (rows // BAND) - OWN // BAND + b
        inside = jnp.where((band >= 0) & (band < bands), 1.0, 0.0).astype(jnp.float32)
        kid = band_ref[jnp.clip(band, 0, bands - 1)]
        row_taps = [jnp.full((BAND, TILE), kern_ref[kid, j], jnp.float32) for j in range(5)]
        total = row_taps[0] + row_taps[1] + row_taps[2] + row_taps[3] + row_taps[4]
        for j in range(5):
            taps[j, b * BAND : (b + 1) * BAND, :] = row_taps[j] / total * inside
        outm[b * BAND : (b + 1) * BAND, :] = jnp.full((BAND, TILE), 1.0 - inside, jnp.float32)

    pl.semaphore_wait(barrier, nd - 1)

    def start_halo(s, _):
        for ct in range(ct_n):
            load(s, ct).wait()

        @pl.when(r > 0)
        def _():
            up(s).start()

        @pl.when(r < nr - 1)
        def _():
            down(s).start()

        return 0

    lax.fori_loop(0, nf, start_halo, 0)

    @pl.when(r == 0)
    def _():
        def clear(s, _):
            obs[s, :, :, OWN - HALO : OWN, :] = jnp.zeros((fd, ct_n, HALO, TILE), jnp.float32)
            return 0
        lax.fori_loop(0, nf, clear, 0)

    @pl.when(r == nr - 1)
    def _():
        def clear(s, _):
            obs[s, :, :, OWN + rows : OWN + rows + HALO, :] = jnp.zeros((fd, ct_n, HALO, TILE), jnp.float32)
            return 0
        lax.fori_loop(0, nf, clear, 0)

    mask_copy.wait()
    wide[...] = jnp.zeros_like(wide)
    for h in range(rows):
        wide[h * ct_n : (h + 1) * ct_n, :] = masks[h].astype(jnp.float32)
    wt[...] = jnp.transpose(wide[...])
    rhs[...] = jnp.zeros_like(rhs)
    for m in range(pack):
        rhs[m, m * slot + frames : m * slot + frames + 1, :] = jnp.ones((1, TILE), jnp.float32)

    def restore(s, ff, store):
        for it in range(ITERS):
            source = obs.at[s, ff] if it == 0 else cur.at[ff]
            reach = HALO - 2 * REACH * it
            lo = OWN - reach + REACH
            hi = OWN + rows + reach - REACH
            for a in range(lo, hi, 8):
                blurred = outm[a : a + 8, :][None] + taps[0, a : a + 8, :][None] * source[:, pl.ds(a - 2, 8), :]
                for j in range(1, 5):
                    blurred = blurred + taps[j, a : a + 8, :][None] * source[:, pl.ds(a + j - 2, 8), :]
                quo[ff, :, pl.ds(a, 8), :] = obs[s, ff, :, pl.ds(a, 8), :] / blurred
            last = it == ITERS - 1
            lo, hi = lo + REACH, hi - REACH
            step = hi - lo if last else 8
            for a in range(lo, hi, step):
                back = None
                for j in range(5):
                    at = a + 2 - j
                    term = taps[j, at : at + step, :][None] * quo[ff, :, pl.ds(at, step), :]
                    back = term if back is None else back + term
                value = source[:, pl.ds(a, step), :] * back
                if last:
                    store(value.astype(jnp.bfloat16))
                else:
                    cur[ff, :, pl.ds(a, step), :] = value

    def wait_halo(s):
        @pl.when(r > 0)
        def _():
            down(s).wait_recv()

        @pl.when(r < nr - 1)
        def _():
            up(s).wait_recv()

    def remote_chunk(s, _):
        wait_halo(s)

        def one(ff, _):
            def store(value):
                for ct in range(ct_n):
                    send[s, ff, :, ct * TILE : (ct + 1) * TILE] = value[ct]
            restore(s, ff, store)
            return 0

        lax.fori_loop(0, fd, one, 0)
        frame_copy(s).start()
        return 0

    lax.fori_loop(0, nf - 1, remote_chunk, 0)
    own = nf - 1
    wait_halo(own)

    def one(ff, _):
        def store(value):
            for ct in range(ct_n):
                est[f, ff, :, ct * TILE : (ct + 1) * TILE] = value[ct]
        restore(own, ff, store)
        return 0

    lax.fori_loop(0, fd, one, 0)

    def frame_recv(s, _):
        frame_wait(s).wait_recv()
        return 0

    lax.fori_loop(0, nf - 1, frame_recv, 0)

    inverse, upper = thomas_factors(frames)
    for ct in range(ct_n):
        cols = slice(ct * TILE, (ct + 1) * TILE)
        value = [est[t // fd, t % fd, :, cols].astype(jnp.float32) for t in range(frames)]
        swept = []
        for t in range(frames):
            right = value[t] if t == 0 else value[t] + SMOOTHING * swept[-1]
            swept.append(right * inverse[t])
        base = [None] * frames
        for t in reversed(range(frames)):
            base[t] = swept[t] if t == frames - 1 else swept[t] - upper[t] * base[t + 1]
        earlier = None
        for t in range(frames):
            detrended = value[t] - base[t]
            out = detrended if t == 0 else detrended - DECAY_RATE * earlier
            spikes_ref[t, :, cols] = out.astype(jnp.bfloat16)
            earlier = detrended

    pixel_tile = lax.broadcasted_iota(jnp.int32, (cpd, TILE), 0) // TILE
    lane = lax.broadcasted_iota(jnp.int32, (cpd, TILE), 1)
    picks = jnp.where(pixel_tile == lane % ct_n, 1.0, 0.0).astype(jnp.bfloat16)
    sums = jnp.dot(
        spikes_ref[...].reshape(frames * rows, cpd), picks, preferred_element_type=jnp.float32
    ).reshape(frames, rows, TILE)
    row_id = lax.broadcasted_iota(jnp.int32, (rows, TILE), 0)
    row_lane = lax.broadcasted_iota(jnp.int32, (rows, TILE), 1)
    tile_sums = jnp.sum(jnp.where((row_id == row_lane // ct_n)[None], sums, 0.0), axis=1)
    total = None
    for m in range(pack):
        rhs[m, m * slot : m * slot + frames, :] = tile_sums
        left = wt[pl.ds(m, comps // pack, stride=pack), :] if pack > 1 else wt[...]
        term = lax.dot_general(
            left, rhs[m], (((1,), (1,)), ((), ())),
            precision=lax.Precision.HIGHEST, preferred_element_type=jnp.float32,
        )
        total = term if total is None else total + term
    for d in range(nd):
        part[d] = total[d * kq : (d + 1) * kq, :]

    def send_part(off, _):
        part_copy(off).start()
        return 0

    lax.fori_loop(1, nd, send_part, 0)
    gath[me] = part[me]

    def recv_part(off, _):
        part_wait(off).wait_recv()
        return 0

    lax.fori_loop(1, nd, recv_part, 0)
    summed = jnp.sum(gath[...], axis=0)
    for m in range(pack):
        piece = summed[:, m * slot : m * slot + frames]
        count = summed[:, m * slot + frames : m * slot + frames + 1]
        answer = piece / (TILE * count)
        for q in range(kq):
            traces_ref[q * pack + m : q * pack + m + 1, :] = answer[q : q + 1, :]

    def drain(s, _):
        frame_copy(s).wait_send()
        return 0

    lax.fori_loop(0, nf - 1, drain, 0)

    def drain_halo(s, _):
        @pl.when(r > 0)
        def _():
            up(s).wait_send()

        @pl.when(r < nr - 1)
        def _():
            down(s).wait_send()

        return 0

    lax.fori_loop(0, nf, drain_halo, 0)

    def drain_part(off, _):
        part_copy(off).wait_send()
        return 0

    lax.fori_loop(1, nd, drain_part, 0)


def rhs_slot(frames):
    slot = 32
    while slot < frames + 1:
        slot *= 2
    return slot


def local(observed, kernels, band_kernel, masks):
    fd, rows, width = observed.shape
    nf = lax.axis_size("frame")
    nr = lax.axis_size("row")
    frames = fd * nf
    cpd = width // nf
    ct_n = cpd // TILE
    comps = masks.shape[0]
    nd = nf * nr
    brows = rows + 2 * OWN
    slot = rhs_slot(frames)
    pack = TILE // slot
    kdev = comps // nd
    f32, bf16 = jnp.float32, jnp.bfloat16
    dma = pltpu.SemaphoreType.DMA
    return pl.pallas_call(
        functools.partial(body, (nf, nr, fd, rows, cpd, comps)),
        out_shape=(
            jax.ShapeDtypeStruct((frames, rows, cpd), bf16),
            jax.ShapeDtypeStruct((kdev, frames), f32),
        ),
        in_specs=[
            pl.BlockSpec(memory_space=pl.ANY),
            pl.BlockSpec(memory_space=pltpu.SMEM),
            pl.BlockSpec(memory_space=pltpu.SMEM),
            pl.BlockSpec(memory_space=pl.ANY),
        ],
        out_specs=(
            pl.BlockSpec(memory_space=pltpu.VMEM),
            pl.BlockSpec(memory_space=pltpu.VMEM),
        ),
        scratch_shapes=[
            pltpu.VMEM((nf, fd, ct_n, brows, TILE), f32),
            pltpu.VMEM((fd, ct_n, brows, TILE), f32),
            pltpu.VMEM((fd, ct_n, brows, TILE), f32),
            pltpu.VMEM((5, brows, TILE), f32),
            pltpu.VMEM((brows, TILE), f32),
            pltpu.VMEM((nf, fd, rows, cpd), bf16),
            pltpu.VMEM((nf, fd, rows, cpd), bf16),
            pltpu.VMEM((rows, ct_n, comps), jnp.int32),
            pltpu.VMEM((TILE, comps), f32),
            pltpu.VMEM((comps, TILE), f32),
            pltpu.VMEM((pack, TILE, TILE), f32),
            pltpu.VMEM((nd, kdev // pack, TILE), f32),
            pltpu.VMEM((nd, kdev // pack, TILE), f32),
            dma((nf, ct_n)),
            dma,
            dma((2, nf)),
            dma((2, nf)),
            dma((nf,)),
            dma((nf,)),
            dma((nd,)),
            dma((nd,)),
        ],
        compiler_params=pltpu.CompilerParams(collective_id=0, has_side_effects=True),
        name="restore_all",
    )(observed, kernels, band_kernel, jnp.transpose(masks, (1, 2, 0)))


def solution(mesh):
    in_specs = (
        P("frame", ("groups", "row"), None),
        P(),
        P("groups"),
        P(None, ("groups", "row"), "frame"),
    )
    out_specs = (P(None, ("groups", "row"), "frame"), P(("groups", "frame", "row"), None))
    return jax.shard_map(local, mesh=mesh, in_specs=in_specs, out_specs=out_specs, check_vma=False)
```

```python
import functools
import jax
import jax.numpy as jnp
from jax import lax
from jax.experimental import pallas as pl
from jax.experimental.pallas import tpu as pltpu
from jax.sharding import PartitionSpec as P

TILE = 128
BAND = 8
ITERS = 3
REACH = 2
HALO = 2 * REACH * ITERS
NEAR = 2 * REACH
FAR = HALO - NEAR
OWN = 16

SMOOTHING = 1024.0
DECAY_RATE = 0.9


def thomas_factors(frames):
    inverse, upper = [], []
    for t in range(frames):
        diag = 1.0 + SMOOTHING * (1.0 if t in (0, frames - 1) else 2.0)
        pivot = diag if t == 0 else diag + SMOOTHING * upper[-1]
        inverse.append(1.0 / pivot)
        upper.append(-SMOOTHING / pivot)
    return inverse, upper


def body(cfg, obs_hbm, kern_ref, band_ref, masks_hbm, spikes_ref, traces_ref,
         obs, far_out, far_in, cur, quo, taps, outm, send, est, masks, wide, wt, rhs, part, gath,
         load_sem, mask_sem, zs, zr, fs, fr, rs, rr):
    nf, nr, fd, rows, cpd, comps = cfg
    ct_n = cpd // TILE
    frames = fd * nf
    nd = nf * nr
    brows = rows + 2 * OWN
    slot = rhs_slot(frames)
    pack = TILE // slot
    kdev = comps // nd
    kq = kdev // pack
    f = lax.axis_index("frame")
    r = lax.axis_index("row")
    me = f * nr + r

    def chunk_of(s):
        dx = s // 2 + 1
        return ((f // 2 + dx) % (nf // 2)) * 2 + (f % 2 + 1 + s) % 2

    def load(s, ct):
        col = pl.multiple_of(chunk_of(s) * cpd + ct * TILE, TILE)
        return pltpu.make_async_copy(
            obs_hbm.at[:, :, pl.ds(col, TILE)],
            obs.at[s, :, ct, OWN : OWN + rows, :],
            load_sem.at[s, ct],
        )

    near_rows = ((OWN, OWN + rows), (OWN + rows - NEAR, OWN - NEAR))
    far_rows = ((OWN + NEAR, OWN + rows + NEAR), (OWN + rows - HALO, OWN - HALO))

    def halo(s, way):
        there = {"row": r - 1 + 2 * way}
        first, put = near_rows[way]
        near = pltpu.make_async_remote_copy(
            src_ref=obs.at[s, :, :, first : first + NEAR, :],
            dst_ref=obs.at[s, :, :, put : put + NEAR, :],
            send_sem=zs.at[way, s],
            recv_sem=zr.at[way, s],
            device_id=there,
            device_id_type=pl.DeviceIdType.MESH,
        )
        far = pltpu.make_async_remote_copy(
            src_ref=far_out.at[way, s],
            dst_ref=far_in.at[way, s],
            send_sem=zs.at[2 + way, s],
            recv_sem=zr.at[2 + way, s],
            device_id=there,
            device_id_type=pl.DeviceIdType.MESH,
        )
        return near, far

    def frame_copy(s):
        c = chunk_of(s)
        return pltpu.make_async_remote_copy(
            src_ref=send.at[s],
            dst_ref=est.at[f],
            send_sem=fs.at[s],
            recv_sem=fr.at[f],
            device_id={"frame": c},
            device_id_type=pl.DeviceIdType.MESH,
        )

    def frame_wait(s):
        c = chunk_of(s)
        return pltpu.make_async_remote_copy(
            src_ref=send.at[s],
            dst_ref=est.at[c],
            send_sem=fs.at[s],
            recv_sem=fr.at[c],
            device_id={"frame": c},
            device_id_type=pl.DeviceIdType.MESH,
        )

    def part_copy(off):
        d = (me + off) % nd
        return pltpu.make_async_remote_copy(
            src_ref=part.at[d],
            dst_ref=gath.at[me],
            send_sem=rs.at[d],
            recv_sem=rr.at[me],
            device_id={"frame": d // nr, "row": d % nr},
            device_id_type=pl.DeviceIdType.MESH,
        )

    def part_wait(off):
        d = (me + off) % nd
        return pltpu.make_async_remote_copy(
            src_ref=part.at[d],
            dst_ref=gath.at[d],
            send_sem=rs.at[d],
            recv_sem=rr.at[d],
            device_id={"frame": d // nr, "row": d % nr},
            device_id_type=pl.DeviceIdType.MESH,
        )

    barrier = pltpu.get_barrier_semaphore()

    def greet(off, _):
        d = (me + off) % nd
        pl.semaphore_signal(
            barrier, inc=1, device_id={"frame": d // nr, "row": d % nr},
            device_id_type=pl.DeviceIdType.MESH,
        )
        return 0

    lax.fori_loop(1, nd, greet, 0)

    def start_loads(s, _):
        for ct in range(ct_n):
            load(s, ct).start()
        return 0

    lax.fori_loop(0, nf, start_loads, 0)
    mask_copy = pltpu.make_async_copy(masks_hbm, masks, mask_sem)
    mask_copy.start()

    bands = band_ref.shape[0]
    for b in range(brows // BAND):
        band = r * (rows // BAND) - OWN // BAND + b
        inside = jnp.where((band >= 0) & (band < bands), 1.0, 0.0).astype(jnp.float32)
        kid = band_ref[jnp.clip(band, 0, bands - 1)]
        row_taps = [jnp.full((BAND, TILE), kern_ref[kid, j], jnp.float32) for j in range(5)]
        total = row_taps[0] + row_taps[1] + row_taps[2] + row_taps[3] + row_taps[4]
        for j in range(5):
            taps[j, b * BAND : (b + 1) * BAND, :] = row_taps[j] / total * inside
        outm[b * BAND : (b + 1) * BAND, :] = jnp.full((BAND, TILE), 1.0 - inside, jnp.float32)

    pl.semaphore_wait(barrier, nd - 1)

    def start_halo(s, _):
        for ct in range(ct_n):
            load(s, ct).wait()

        for way in range(2):
            @pl.when((r > 0) if way == 0 else (r < nr - 1))
            def _():
                near, far = halo(s, way)
                near.start()
                first = far_rows[way][0]
                for ff in range(fd):
                    values = obs[s, ff, :, pl.ds(first, FAR), :].reshape(ct_n * FAR, TILE)
                    far_out[way, s, ff] = values.astype(jnp.bfloat16)
                far.start()

        return 0

    lax.fori_loop(0, nf, start_halo, 0)

    @pl.when(r == 0)
    def _():
        def clear(s, _):
            obs[s, :, :, OWN - HALO : OWN, :] = jnp.zeros((fd, ct_n, HALO, TILE), jnp.float32)
            return 0
        lax.fori_loop(0, nf, clear, 0)

    @pl.when(r == nr - 1)
    def _():
        def clear(s, _):
            obs[s, :, :, OWN + rows : OWN + rows + HALO, :] = jnp.zeros((fd, ct_n, HALO, TILE), jnp.float32)
            return 0
        lax.fori_loop(0, nf, clear, 0)

    mask_copy.wait()
    wide[...] = jnp.zeros_like(wide)
    for h in range(rows):
        wide[h * ct_n : (h + 1) * ct_n, :] = masks[h].astype(jnp.float32)
    wt[...] = jnp.transpose(wide[...])
    rhs[...] = jnp.zeros_like(rhs)
    for m in range(pack):
        rhs[m, m * slot + frames : m * slot + frames + 1, :] = jnp.ones((1, TILE), jnp.float32)

    def restore(s, ff, store):
        for it in range(ITERS):
            source = obs.at[s, ff] if it == 0 else cur.at[ff]
            reach = HALO - 2 * REACH * it
            lo = OWN - reach + REACH
            hi = OWN + rows + reach - REACH
            for a in range(lo, hi, 8):
                blurred = outm[a : a + 8, :][None] + taps[0, a : a + 8, :][None] * source[:, pl.ds(a - 2, 8), :]
                for j in range(1, 5):
                    blurred = blurred + taps[j, a : a + 8, :][None] * source[:, pl.ds(a + j - 2, 8), :]
                quo[ff, :, pl.ds(a, 8), :] = obs[s, ff, :, pl.ds(a, 8), :] / blurred
            last = it == ITERS - 1
            lo, hi = lo + REACH, hi - REACH
            step = hi - lo if last else 8
            for a in range(lo, hi, step):
                back = None
                for j in range(5):
                    at = a + 2 - j
                    term = taps[j, at : at + step, :][None] * quo[ff, :, pl.ds(at, step), :]
                    back = term if back is None else back + term
                value = source[:, pl.ds(a, step), :] * back
                if last:
                    store(value.astype(jnp.bfloat16))
                else:
                    cur[ff, :, pl.ds(a, step), :] = value

    def wait_halo(s):
        for way in range(2):
            @pl.when((r < nr - 1) if way == 0 else (r > 0))
            def _():
                near, far = halo(s, way)
                near.wait_recv()
                far.wait_recv()
                put = far_rows[way][1]
                for ff in range(fd):
                    values = far_in[way, s, ff].astype(jnp.float32)
                    obs[s, ff, :, pl.ds(put, FAR), :] = values.reshape(ct_n, FAR, TILE)

    def remote_chunk(s, _):
        wait_halo(s)

        def one(ff, _):
            def store(value):
                for ct in range(ct_n):
                    send[s, ff, :, ct * TILE : (ct + 1) * TILE] = value[ct]
            restore(s, ff, store)
            return 0

        lax.fori_loop(0, fd, one, 0)
        frame_copy(s).start()
        return 0

    lax.fori_loop(0, nf - 1, remote_chunk, 0)
    own = nf - 1
    wait_halo(own)

    def one(ff, _):
        def store(value):
            for ct in range(ct_n):
                est[f, ff, :, ct * TILE : (ct + 1) * TILE] = value[ct]
        restore(own, ff, store)
        return 0

    lax.fori_loop(0, fd, one, 0)

    def frame_recv(s, _):
        frame_wait(s).wait_recv()
        return 0

    lax.fori_loop(0, nf - 1, frame_recv, 0)

    inverse, upper = thomas_factors(frames)
    for ct in range(ct_n):
        cols = slice(ct * TILE, (ct + 1) * TILE)
        value = [est[t // fd, t % fd, :, cols].astype(jnp.float32) for t in range(frames)]
        swept = []
        for t in range(frames):
            right = value[t] if t == 0 else value[t] + SMOOTHING * swept[-1]
            swept.append(right * inverse[t])
        base = [None] * frames
        for t in reversed(range(frames)):
            base[t] = swept[t] if t == frames - 1 else swept[t] - upper[t] * base[t + 1]
        earlier = None
        for t in range(frames):
            detrended = value[t] - base[t]
            out = detrended if t == 0 else detrended - DECAY_RATE * earlier
            spikes_ref[t, :, cols] = out.astype(jnp.bfloat16)
            earlier = detrended

    pixel_tile = lax.broadcasted_iota(jnp.int32, (cpd, TILE), 0) // TILE
    lane = lax.broadcasted_iota(jnp.int32, (cpd, TILE), 1)
    picks = jnp.where(pixel_tile == lane % ct_n, 1.0, 0.0).astype(jnp.bfloat16)
    sums = jnp.dot(
        spikes_ref[...].reshape(frames * rows, cpd), picks, preferred_element_type=jnp.float32
    ).reshape(frames, rows, TILE)
    row_id = lax.broadcasted_iota(jnp.int32, (rows, TILE), 0)
    row_lane = lax.broadcasted_iota(jnp.int32, (rows, TILE), 1)
    tile_sums = jnp.sum(jnp.where((row_id == row_lane // ct_n)[None], sums, 0.0), axis=1)
    total = None
    for m in range(pack):
        rhs[m, m * slot : m * slot + frames, :] = tile_sums
        left = wt[pl.ds(m, comps // pack, stride=pack), :] if pack > 1 else wt[...]
        term = lax.dot_general(
            left, rhs[m], (((1,), (1,)), ((), ())),
            precision=lax.Precision.HIGHEST, preferred_element_type=jnp.float32,
        )
        total = term if total is None else total + term
    for d in range(nd):
        part[d] = total[d * kq : (d + 1) * kq, :]

    def send_part(off, _):
        part_copy(off).start()
        return 0

    lax.fori_loop(1, nd, send_part, 0)
    gath[me] = part[me]

    def recv_part(off, _):
        part_wait(off).wait_recv()
        return 0

    lax.fori_loop(1, nd, recv_part, 0)
    summed = jnp.sum(gath[...], axis=0)
    for m in range(pack):
        piece = summed[:, m * slot : m * slot + frames]
        count = summed[:, m * slot + frames : m * slot + frames + 1]
        answer = piece / (TILE * count)
        for q in range(kq):
            traces_ref[q * pack + m : q * pack + m + 1, :] = answer[q : q + 1, :]

    def drain(s, _):
        frame_copy(s).wait_send()
        return 0

    lax.fori_loop(0, nf - 1, drain, 0)

    def drain_halo(s, _):
        for way in range(2):
            @pl.when((r > 0) if way == 0 else (r < nr - 1))
            def _():
                near, far = halo(s, way)
                near.wait_send()
                far.wait_send()

        return 0

    lax.fori_loop(0, nf, drain_halo, 0)

    def drain_part(off, _):
        part_copy(off).wait_send()
        return 0

    lax.fori_loop(1, nd, drain_part, 0)


def rhs_slot(frames):
    slot = 32
    while slot < frames + 1:
        slot *= 2
    return slot


def local(observed, kernels, band_kernel, masks):
    fd, rows, width = observed.shape
    nf = lax.axis_size("frame")
    nr = lax.axis_size("row")
    frames = fd * nf
    cpd = width // nf
    ct_n = cpd // TILE
    comps = masks.shape[0]
    nd = nf * nr
    brows = rows + 2 * OWN
    slot = rhs_slot(frames)
    pack = TILE // slot
    kdev = comps // nd
    f32, bf16 = jnp.float32, jnp.bfloat16
    dma = pltpu.SemaphoreType.DMA
    spikes, traces = pl.pallas_call(
        functools.partial(body, (nf, nr, fd, rows, cpd, comps)),
        out_shape=(
            pltpu.VMEM((frames, rows, cpd), bf16),
            pltpu.VMEM((kdev, frames), f32),
        ),
        in_specs=[
            pl.BlockSpec(memory_space=pl.ANY),
            pl.BlockSpec(memory_space=pltpu.SMEM),
            pl.BlockSpec(memory_space=pltpu.SMEM),
            pl.BlockSpec(memory_space=pl.ANY),
        ],
        out_specs=(
            pl.BlockSpec(memory_space=pltpu.VMEM),
            pl.BlockSpec(memory_space=pltpu.VMEM),
        ),
        scratch_shapes=[
            pltpu.VMEM((nf, fd, ct_n, brows, TILE), f32),
            pltpu.VMEM((2, nf, fd, ct_n * FAR, TILE), bf16),
            pltpu.VMEM((2, nf, fd, ct_n * FAR, TILE), bf16),
            pltpu.VMEM((fd, ct_n, brows, TILE), f32),
            pltpu.VMEM((fd, ct_n, brows, TILE), f32),
            pltpu.VMEM((5, brows, TILE), f32),
            pltpu.VMEM((brows, TILE), f32),
            pltpu.VMEM((nf, fd, rows, cpd), bf16),
            pltpu.VMEM((nf, fd, rows, cpd), bf16),
            pltpu.VMEM((rows, ct_n, comps), jnp.int32),
            pltpu.VMEM((TILE, comps), f32),
            pltpu.VMEM((comps, TILE), f32),
            pltpu.VMEM((pack, TILE, TILE), f32),
            pltpu.VMEM((nd, kdev // pack, TILE), f32),
            pltpu.VMEM((nd, kdev // pack, TILE), f32),
            dma((nf, ct_n)),
            dma,
            dma((4, nf)),
            dma((4, nf)),
            dma((nf,)),
            dma((nf,)),
            dma((nd,)),
            dma((nd,)),
        ],
        compiler_params=pltpu.CompilerParams(collective_id=0, has_side_effects=True),
        name="restore_all",
    )(observed, kernels, band_kernel, jnp.transpose(masks, (1, 2, 0)))
    return pl.pallas_call(
        write_out,
        out_shape=(
            jax.ShapeDtypeStruct((frames, rows, cpd), bf16),
            jax.ShapeDtypeStruct((kdev, frames), f32),
        ),
        in_specs=[pl.BlockSpec(memory_space=pltpu.VMEM)] * 2,
        out_specs=(pl.BlockSpec(memory_space=pl.ANY),) * 2,
        scratch_shapes=[dma, dma],
        name="write_out",
    )(
        pltpu.with_memory_space_constraint(spikes, pltpu.VMEM),
        pltpu.with_memory_space_constraint(traces, pltpu.VMEM),
    )


def write_out(spikes_ref, traces_ref, spikes_out, traces_out, spikes_sem, traces_sem):
    big = pltpu.make_async_copy(spikes_ref, spikes_out, spikes_sem)
    small = pltpu.make_async_copy(traces_ref, traces_out, traces_sem)
    big.start()
    small.start()
    big.wait()
    small.wait()


def solution(mesh):
    in_specs = (
        P("frame", ("groups", "row"), None),
        P(),
        P("groups"),
        P(None, ("groups", "row"), "frame"),
    )
    out_specs = (P(None, ("groups", "row"), "frame"), P(("groups", "frame", "row"), None))
    return jax.shard_map(local, mesh=mesh, in_specs=in_specs, out_specs=out_specs, check_vma=False)
```

```python
import functools
import jax
import jax.numpy as jnp
from jax import lax
from jax.experimental import pallas as pl
from jax.experimental.pallas import tpu as pltpu
from jax.sharding import PartitionSpec as P

TILE = 128
BAND = 8
ITERS = 3
REACH = 2
HALO = 2 * REACH * ITERS
NEAR = 2 * REACH
FAR = HALO - NEAR
OWN = 16

SMOOTHING = 1024.0
DECAY_RATE = 0.9


def thomas_factors(frames):
    inverse, upper = [], []
    for t in range(frames):
        diag = 1.0 + SMOOTHING * (1.0 if t in (0, frames - 1) else 2.0)
        pivot = diag if t == 0 else diag + SMOOTHING * upper[-1]
        inverse.append(1.0 / pivot)
        upper.append(-SMOOTHING / pivot)
    return inverse, upper


def body(cfg, obs_hbm, kern_ref, band_ref, masks_hbm, spikes_ref, traces_ref,
         obs, far_out, far_in, cur, quo, taps, outm, send, est, masks, wide, wt, rhs, part, gath,
         load_sem, mask_sem, zs, zr, fs, fr, rs, rr, chain):
    nf, nr, fd, rows, cpd, comps = cfg
    ct_n = cpd // TILE
    frames = fd * nf
    nd = nf * nr
    brows = rows + 2 * OWN
    slot = rhs_slot(frames)
    pack = TILE // slot
    kdev = comps // nd
    kq = kdev // pack
    f = lax.axis_index("frame")
    r = lax.axis_index("row")
    me = f * nr + r

    def chunk_of(s):
        dx = s // 2 + 1
        return ((f // 2 + dx) % (nf // 2)) * 2 + (f % 2 + 1 + s) % 2

    def load(s, ct):
        col = pl.multiple_of(chunk_of(s) * cpd + ct * TILE, TILE)
        return pltpu.make_async_copy(
            obs_hbm.at[:, :, pl.ds(col, TILE)],
            obs.at[s, :, ct, OWN : OWN + rows, :],
            load_sem.at[s, ct],
        )

    near_rows = ((OWN, OWN + rows), (OWN + rows - NEAR, OWN - NEAR))
    far_rows = ((OWN + NEAR, OWN + rows + NEAR), (OWN + rows - HALO, OWN - HALO))

    def halo(s, way):
        there = {"row": r - 1 + 2 * way}
        first, put = near_rows[way]
        near = pltpu.make_async_remote_copy(
            src_ref=obs.at[s, :, :, first : first + NEAR, :],
            dst_ref=obs.at[s, :, :, put : put + NEAR, :],
            send_sem=zs.at[way, s],
            recv_sem=zr.at[way, s],
            device_id=there,
            device_id_type=pl.DeviceIdType.MESH,
        )
        far = pltpu.make_async_remote_copy(
            src_ref=far_out.at[way, s],
            dst_ref=far_in.at[way, s],
            send_sem=zs.at[2 + way, s],
            recv_sem=zr.at[2 + way, s],
            device_id=there,
            device_id_type=pl.DeviceIdType.MESH,
        )
        return near, far

    def frame_copy(s):
        c = chunk_of(s)
        return pltpu.make_async_remote_copy(
            src_ref=send.at[s],
            dst_ref=est.at[f],
            send_sem=fs.at[s],
            recv_sem=fr.at[f],
            device_id={"frame": c},
            device_id_type=pl.DeviceIdType.MESH,
        )

    def frame_wait(s):
        c = chunk_of(s)
        return pltpu.make_async_remote_copy(
            src_ref=send.at[s],
            dst_ref=est.at[c],
            send_sem=fs.at[s],
            recv_sem=fr.at[c],
            device_id={"frame": c},
            device_id_type=pl.DeviceIdType.MESH,
        )

    def part_copy(off):
        d = (me + off) % nd
        return pltpu.make_async_remote_copy(
            src_ref=part.at[d],
            dst_ref=gath.at[me],
            send_sem=rs.at[d],
            recv_sem=rr.at[me],
            device_id={"frame": d // nr, "row": d % nr},
            device_id_type=pl.DeviceIdType.MESH,
        )

    def part_wait(off):
        d = (me + off) % nd
        return pltpu.make_async_remote_copy(
            src_ref=part.at[d],
            dst_ref=gath.at[d],
            send_sem=rs.at[d],
            recv_sem=rr.at[d],
            device_id={"frame": d // nr, "row": d % nr},
            device_id_type=pl.DeviceIdType.MESH,
        )

    barrier = pltpu.get_barrier_semaphore()

    for way in range(2):
        @pl.when((r > 0) if way == 0 else (r < nr - 1))
        def _():
            pl.semaphore_signal(
                barrier, inc=1, device_id={"row": r - 1 + 2 * way},
                device_id_type=pl.DeviceIdType.MESH,
            )

    def greet(off, _):
        pl.semaphore_signal(
            barrier, inc=1, device_id={"frame": (f + off) % nf},
            device_id_type=pl.DeviceIdType.MESH,
        )
        return 0

    lax.fori_loop(1, nf, greet, 0)

    def start_loads(s, _):
        for ct in range(ct_n):
            load(s, ct).start()
        return 0

    lax.fori_loop(0, nf, start_loads, 0)
    mask_copy = pltpu.make_async_copy(masks_hbm, masks, mask_sem)
    mask_copy.start()

    bands = band_ref.shape[0]
    for b in range(brows // BAND):
        band = r * (rows // BAND) - OWN // BAND + b
        inside = jnp.where((band >= 0) & (band < bands), 1.0, 0.0).astype(jnp.float32)
        kid = band_ref[jnp.clip(band, 0, bands - 1)]
        row_taps = [jnp.full((BAND, TILE), kern_ref[kid, j], jnp.float32) for j in range(5)]
        total = row_taps[0] + row_taps[1] + row_taps[2] + row_taps[3] + row_taps[4]
        for j in range(5):
            taps[j, b * BAND : (b + 1) * BAND, :] = row_taps[j] / total * inside
        outm[b * BAND : (b + 1) * BAND, :] = jnp.full((BAND, TILE), 1.0 - inside, jnp.float32)

    peers = nf - 1 + (r > 0).astype(jnp.int32) + (r < nr - 1).astype(jnp.int32)
    pl.semaphore_wait(barrier, peers)

    def start_halo(s, _):
        for ct in range(ct_n):
            load(s, ct).wait()

        for way in range(2):
            @pl.when((r > 0) if way == 0 else (r < nr - 1))
            def _():
                near, far = halo(s, way)
                near.start()
                first = far_rows[way][0]
                for ff in range(fd):
                    values = obs[s, ff, :, pl.ds(first, FAR), :].reshape(ct_n * FAR, TILE)
                    far_out[way, s, ff] = values.astype(jnp.bfloat16)
                far.start()

        return 0

    lax.fori_loop(0, nf, start_halo, 0)

    @pl.when(r == 0)
    def _():
        def clear(s, _):
            obs[s, :, :, OWN - HALO : OWN, :] = jnp.zeros((fd, ct_n, HALO, TILE), jnp.float32)
            return 0
        lax.fori_loop(0, nf, clear, 0)

    @pl.when(r == nr - 1)
    def _():
        def clear(s, _):
            obs[s, :, :, OWN + rows : OWN + rows + HALO, :] = jnp.zeros((fd, ct_n, HALO, TILE), jnp.float32)
            return 0
        lax.fori_loop(0, nf, clear, 0)

    mask_copy.wait()
    wide[...] = jnp.zeros_like(wide)
    for h in range(rows):
        wide[h * ct_n : (h + 1) * ct_n, :] = masks[h].astype(jnp.float32)
    wt[...] = jnp.transpose(wide[...])
    rhs[...] = jnp.zeros_like(rhs)
    for m in range(pack):
        rhs[m, m * slot + frames : m * slot + frames + 1, :] = jnp.ones((1, TILE), jnp.float32)

    for way in range(2):
        behind, ahead = ((r > 0), (r < nr - 1)) if way == 0 else ((r < nr - 1), (r > 0))

        @pl.when(behind)
        def _():
            pl.semaphore_wait(chain.at[way], 1)

        @pl.when(ahead)
        def _():
            pl.semaphore_signal(
                chain.at[way], inc=1, device_id={"row": r + 1 - 2 * way},
                device_id_type=pl.DeviceIdType.MESH,
            )

    def restore(s, ff, store):
        for it in range(ITERS):
            source = obs.at[s, ff] if it == 0 else cur.at[ff]
            reach = HALO - 2 * REACH * it
            lo = OWN - reach + REACH
            hi = OWN + rows + reach - REACH
            for a in range(lo, hi, 8):
                blurred = outm[a : a + 8, :][None] + taps[0, a : a + 8, :][None] * source[:, pl.ds(a - 2, 8), :]
                for j in range(1, 5):
                    blurred = blurred + taps[j, a : a + 8, :][None] * source[:, pl.ds(a + j - 2, 8), :]
                quo[ff, :, pl.ds(a, 8), :] = obs[s, ff, :, pl.ds(a, 8), :] / blurred
            last = it == ITERS - 1
            lo, hi = lo + REACH, hi - REACH
            step = hi - lo if last else 8
            for a in range(lo, hi, step):
                back = None
                for j in range(5):
                    at = a + 2 - j
                    term = taps[j, at : at + step, :][None] * quo[ff, :, pl.ds(at, step), :]
                    back = term if back is None else back + term
                value = source[:, pl.ds(a, step), :] * back
                if last:
                    store(value.astype(jnp.bfloat16))
                else:
                    cur[ff, :, pl.ds(a, step), :] = value

    def wait_halo(s):
        for way in range(2):
            @pl.when((r < nr - 1) if way == 0 else (r > 0))
            def _():
                near, far = halo(s, way)
                near.wait_recv()
                far.wait_recv()
                put = far_rows[way][1]
                for ff in range(fd):
                    values = far_in[way, s, ff].astype(jnp.float32)
                    obs[s, ff, :, pl.ds(put, FAR), :] = values.reshape(ct_n, FAR, TILE)

    def remote_chunk(s, _):
        wait_halo(s)

        def one(ff, _):
            def store(value):
                for ct in range(ct_n):
                    send[s, ff, :, ct * TILE : (ct + 1) * TILE] = value[ct]
            restore(s, ff, store)
            return 0

        lax.fori_loop(0, fd, one, 0)
        frame_copy(s).start()
        return 0

    lax.fori_loop(0, nf - 1, remote_chunk, 0)
    own = nf - 1
    wait_halo(own)

    def one(ff, _):
        def store(value):
            for ct in range(ct_n):
                est[f, ff, :, ct * TILE : (ct + 1) * TILE] = value[ct]
        restore(own, ff, store)
        return 0

    lax.fori_loop(0, fd, one, 0)

    def frame_recv(s, _):
        frame_wait(s).wait_recv()
        return 0

    lax.fori_loop(0, nf - 1, frame_recv, 0)

    inverse, upper = thomas_factors(frames)
    for ct in range(ct_n):
        cols = slice(ct * TILE, (ct + 1) * TILE)
        value = [est[t // fd, t % fd, :, cols].astype(jnp.float32) for t in range(frames)]
        swept = []
        for t in range(frames):
            right = value[t] if t == 0 else value[t] + SMOOTHING * swept[-1]
            swept.append(right * inverse[t])
        base = [None] * frames
        for t in reversed(range(frames)):
            base[t] = swept[t] if t == frames - 1 else swept[t] - upper[t] * base[t + 1]
        earlier = None
        for t in range(frames):
            detrended = value[t] - base[t]
            out = detrended if t == 0 else detrended - DECAY_RATE * earlier
            spikes_ref[t, :, cols] = out.astype(jnp.bfloat16)
            earlier = detrended

    pixel_tile = lax.broadcasted_iota(jnp.int32, (cpd, TILE), 0) // TILE
    lane = lax.broadcasted_iota(jnp.int32, (cpd, TILE), 1)
    picks = jnp.where(pixel_tile == lane % ct_n, 1.0, 0.0).astype(jnp.bfloat16)
    sums = jnp.dot(
        spikes_ref[...].reshape(frames * rows, cpd), picks, preferred_element_type=jnp.float32
    ).reshape(frames, rows, TILE)
    row_id = lax.broadcasted_iota(jnp.int32, (rows, TILE), 0)
    row_lane = lax.broadcasted_iota(jnp.int32, (rows, TILE), 1)
    tile_sums = jnp.sum(jnp.where((row_id == row_lane // ct_n)[None], sums, 0.0), axis=1)
    total = None
    for m in range(pack):
        rhs[m, m * slot : m * slot + frames, :] = tile_sums
        left = wt[pl.ds(m, comps // pack, stride=pack), :] if pack > 1 else wt[...]
        term = lax.dot_general(
            left, rhs[m], (((1,), (1,)), ((), ())),
            precision=lax.Precision.HIGHEST, preferred_element_type=jnp.float32,
        )
        total = term if total is None else total + term
    for d in range(nd):
        part[d] = total[d * kq : (d + 1) * kq, :]

    def send_part(off, _):
        part_copy(off).start()
        return 0

    lax.fori_loop(1, nd, send_part, 0)
    gath[me] = part[me]

    def recv_part(off, _):
        part_wait(off).wait_recv()
        return 0

    lax.fori_loop(1, nd, recv_part, 0)
    summed = jnp.sum(gath[...], axis=0)
    for m in range(pack):
        piece = summed[:, m * slot : m * slot + frames]
        count = summed[:, m * slot + frames : m * slot + frames + 1]
        answer = piece / (TILE * count)
        for q in range(kq):
            traces_ref[q * pack + m : q * pack + m + 1, :] = answer[q : q + 1, :]

    def drain(s, _):
        frame_copy(s).wait_send()
        return 0

    lax.fori_loop(0, nf - 1, drain, 0)

    def drain_halo(s, _):
        for way in range(2):
            @pl.when((r > 0) if way == 0 else (r < nr - 1))
            def _():
                near, far = halo(s, way)
                near.wait_send()
                far.wait_send()

        return 0

    lax.fori_loop(0, nf, drain_halo, 0)

    def drain_part(off, _):
        part_copy(off).wait_send()
        return 0

    lax.fori_loop(1, nd, drain_part, 0)


def rhs_slot(frames):
    slot = 32
    while slot < frames + 1:
        slot *= 2
    return slot


def local(observed, kernels, band_kernel, masks):
    fd, rows, width = observed.shape
    nf = lax.axis_size("frame")
    nr = lax.axis_size("row")
    frames = fd * nf
    cpd = width // nf
    ct_n = cpd // TILE
    comps = masks.shape[0]
    nd = nf * nr
    brows = rows + 2 * OWN
    slot = rhs_slot(frames)
    pack = TILE // slot
    kdev = comps // nd
    f32, bf16 = jnp.float32, jnp.bfloat16
    dma = pltpu.SemaphoreType.DMA
    spikes, traces = pl.pallas_call(
        functools.partial(body, (nf, nr, fd, rows, cpd, comps)),
        out_shape=(
            pltpu.VMEM((frames, rows, cpd), bf16),
            pltpu.VMEM((kdev, frames), f32),
        ),
        in_specs=[
            pl.BlockSpec(memory_space=pl.ANY),
            pl.BlockSpec(memory_space=pltpu.SMEM),
            pl.BlockSpec(memory_space=pltpu.SMEM),
            pl.BlockSpec(memory_space=pl.ANY),
        ],
        out_specs=(
            pl.BlockSpec(memory_space=pltpu.VMEM),
            pl.BlockSpec(memory_space=pltpu.VMEM),
        ),
        scratch_shapes=[
            pltpu.VMEM((nf, fd, ct_n, brows, TILE), f32),
            pltpu.VMEM((2, nf, fd, ct_n * FAR, TILE), bf16),
            pltpu.VMEM((2, nf, fd, ct_n * FAR, TILE), bf16),
            pltpu.VMEM((fd, ct_n, brows, TILE), f32),
            pltpu.VMEM((fd, ct_n, brows, TILE), f32),
            pltpu.VMEM((5, brows, TILE), f32),
            pltpu.VMEM((brows, TILE), f32),
            pltpu.VMEM((nf, fd, rows, cpd), bf16),
            pltpu.VMEM((nf, fd, rows, cpd), bf16),
            pltpu.VMEM((rows, ct_n, comps), jnp.int32),
            pltpu.VMEM((TILE, comps), f32),
            pltpu.VMEM((comps, TILE), f32),
            pltpu.VMEM((pack, TILE, TILE), f32),
            pltpu.VMEM((nd, kdev // pack, TILE), f32),
            pltpu.VMEM((nd, kdev // pack, TILE), f32),
            dma((nf, ct_n)),
            dma,
            dma((4, nf)),
            dma((4, nf)),
            dma((nf,)),
            dma((nf,)),
            dma((nd,)),
            dma((nd,)),
            pltpu.SemaphoreType.REGULAR((2,)),
        ],
        compiler_params=pltpu.CompilerParams(collective_id=0, has_side_effects=True),
        name="restore_all",
    )(observed, kernels, band_kernel, jnp.transpose(masks, (1, 2, 0)))
    return pl.pallas_call(
        write_out,
        out_shape=(
            jax.ShapeDtypeStruct((frames, rows, cpd), bf16),
            jax.ShapeDtypeStruct((kdev, frames), f32),
        ),
        in_specs=[pl.BlockSpec(memory_space=pltpu.VMEM)] * 2,
        out_specs=(pl.BlockSpec(memory_space=pl.ANY),) * 2,
        scratch_shapes=[dma, dma],
        name="write_out",
    )(
        pltpu.with_memory_space_constraint(spikes, pltpu.VMEM),
        pltpu.with_memory_space_constraint(traces, pltpu.VMEM),
    )


def write_out(spikes_ref, traces_ref, spikes_out, traces_out, spikes_sem, traces_sem):
    big = pltpu.make_async_copy(spikes_ref, spikes_out, spikes_sem)
    small = pltpu.make_async_copy(traces_ref, traces_out, traces_sem)
    big.start()
    small.start()
    big.wait()
    small.wait()


def solution(mesh):
    in_specs = (
        P("frame", ("groups", "row"), None),
        P(),
        P("groups"),
        P(None, ("groups", "row"), "frame"),
    )
    out_specs = (P(None, ("groups", "row"), "frame"), P(("groups", "frame", "row"), None))
    return jax.shard_map(local, mesh=mesh, in_specs=in_specs, out_specs=out_specs, check_vma=False)
```
